128 devices in a mesh: clu: 32 (over y, z, core), sub: 4 (over x).
Axes of the slice: x: 4, y: 4, z: 4, core: 2. Of those that a mesh axis runs over, the one named last changes fastest.
Arguments:
- points: bfloat16 [1024, 1024, 128], P('clu', 'sub'), may hold values from -6 to 6
- row_sketch: bfloat16 [32, 32, 1024, 128], P('clu', 'sub'), may hold values from -0.75 to 0.75
- col_sketch: bfloat16 [32, 32, 1024, 128], P('clu', 'sub'), may hold values from -0.75 to 0.75
- pair_count: int32 [32], P('clu'), may hold values from 4 to 32
- pair_local: int32 [32, 32], P('clu'), may hold values from 0 to 31
- pair_src: int32 [32, 32], P('clu'), may hold values from 0 to 31, as said below
- pair_partner: int32 [32, 32], P('clu'), may hold values from 0 to 31
- pair_rank: int32 [32, 32], P('clu'), may hold values from 64 to 128
Outputs:
- row_factor: bfloat16 [32, 32, 1024, 128], P('clu', 'sub')
- col_factor: bfloat16 [32, 32, 2, 1024, 128], P('clu', None, None, 'sub')
The draws below stay inside these ranges and needn't reach their ends.
Inputs may be any that keep to these rules, and one draw needn't show every extreme that they name: `pair_src`: in each group's row every source group appears exactly 2 times or not at all, and its 2 slots p lie in 2 different blocks p // 8.
All inputs are finite; a program needn't handle non-finite values.
Results may differ from the reference program's by a relative error of at most 0.0049.
Values may be sent and summed in bfloat16 or wider, within the bound.
A program may use at most 128 MiB of HBM per device.

```python
import jax
import jax.numpy as jnp
from jax import lax

DIM = 128
CLS = 1024
RMAX = 128
CAP = 2
CPG = 32
GROUPS = 32
PAIRS = 32
PQ = 8
CLUSTERS = 1024
N_SUB = 4


def draw_pair_src(key, part):
    row_keys = jax.random.split(jax.random.fold_in(key, 11), GROUPS)

    def one_row(row_key):
        first_key, second_key, third_key = jax.random.split(row_key, 3)
        chosen = jax.random.permutation(first_key, GROUPS)[:PAIRS // CAP]
        laid = jnp.concatenate([chosen] * CAP).reshape(N_SUB, PQ)
        column_keys = jax.random.split(second_key, N_SUB)
        mixed = jax.vmap(lambda one_key, one_line: one_line[jax.random.permutation(one_key, PQ)])(column_keys, laid)
        mixed = mixed[jax.random.permutation(third_key, N_SUB)]
        return mixed.reshape(PAIRS)
    return jax.vmap(one_row)(row_keys).astype(jnp.int32)


def place_ends(drawn, key, least, high):
    spot = [jax.random.randint(jax.random.fold_in(key, axis), (), 0, length) for axis, length in enumerate(drawn.shape)]
    widest = drawn.shape.index(max(drawn.shape))
    neighbour = spot[:widest] + [(spot[widest] + 1) % drawn.shape[widest]] + spot[widest + 1:]
    return drawn.at[tuple(spot)].set(least).at[tuple(neighbour)].set(high)


def shard_levels(own_key, extent, cuts, smallest, top_value):
    def one(dim, blocks):
        draws = jax.random.uniform(jax.random.fold_in(jax.random.fold_in(own_key, 6), dim), (blocks,), jnp.float32, smallest / len(cuts), top_value / len(cuts))
        return jnp.repeat(jnp.exp(draws), extent[dim] // blocks).reshape((-1,) + (1,) * (len(extent) - dim - 1))

    loudness = one(*cuts[0])
    for cut in cuts[1:]:
        loudness = loudness * one(*cut)
    return loudness


def noise(own_key, extent, spread, most, shards=(), held_as=jnp.bfloat16):
    gain = shard_levels(own_key, extent, shards, -0.22, 0.18) if shards else 1.0
    values = jax.random.normal(own_key, extent, jnp.float32) * spread * gain
    return jnp.minimum(jnp.maximum(values, -most), most).astype(held_as)


def setup_inputs(seed: int = 0) -> dict:
    seeds = jax.random.split(jax.random.key(seed), 9)
    return {
        "points": noise(seeds[0], (CLUSTERS, CLS, DIM), 1.0, 6.0, ((0, 32), (1, 4))),
        "row_sketch": noise(seeds[1], (GROUPS, PAIRS, CLS, RMAX), (CLS // 16) ** -0.5, 0.75, ((0, 32), (1, 4))),
        "col_sketch": noise(seeds[2], (GROUPS, PAIRS, CLS, RMAX), (CLS // 16) ** -0.5, 0.75, ((0, 32), (1, 4))),
        "pair_count": place_ends(jax.random.randint(seeds[3], (GROUPS,), GROUPS // 8, GROUPS + 1), jax.random.fold_in(seeds[3], 1), GROUPS // 8, GROUPS).astype(jnp.int32),
        "pair_local": place_ends(jax.random.randint(seeds[4], (GROUPS, PAIRS), 0, CPG), jax.random.fold_in(seeds[4], 1), 0, CPG - 1).astype(jnp.int32),
        "pair_src": draw_pair_src(jax.random.fold_in(seeds[8], 71), 0),
        "pair_partner": place_ends(jax.random.randint(seeds[6], (GROUPS, PAIRS), 0, CPG), jax.random.fold_in(seeds[6], 1), 0, CPG - 1).astype(jnp.int32),
        "pair_rank": place_ends(jax.random.randint(seeds[7], (GROUPS, PAIRS), RMAX // 2, RMAX + 1), jax.random.fold_in(seeds[7], 1), RMAX // 2, RMAX).astype(jnp.int32),
    }


def kernel_tile(left_points, right_points):
    left_norm = jnp.sum(jnp.square(left_points.astype(jnp.float32)), axis=1)
    right_norm = jnp.sum(jnp.square(right_points.astype(jnp.float32)), axis=1)
    inner_term = jnp.dot(left_points, right_points.T, preferred_element_type=jnp.float32)
    return jnp.exp(-(left_norm[:, None] + right_norm[None, :] - 2.0 * inner_term) / DIM)


def slot_numbers(sources):
    position = jnp.arange(sources.shape[0], dtype=jnp.int32)
    earlier_same = (sources[:, None] == sources[None, :]) & (position[None, :] < position[:, None])
    return jnp.sum(earlier_same.astype(jnp.int32), axis=1).astype(jnp.int32)


def reference(points, row_sketch, col_sketch, pair_count, pair_local, pair_src, pair_partner, pair_rank):
    slot_index = jax.vmap(slot_numbers)(pair_src)
    group_grid = jnp.broadcast_to(jnp.arange(GROUPS, dtype=jnp.int32)[:, None], (GROUPS, PAIRS))
    pair_grid = jnp.broadcast_to(jnp.arange(PAIRS, dtype=jnp.int32)[None, :], (GROUPS, PAIRS))

    def one_pair(pair_item):
        group_id, pair_id = pair_item
        source = pair_src[group_id, pair_id]
        owner_pts = points[group_id * CPG + pair_local[group_id, pair_id]]
        partner_pts = points[source * CPG + pair_partner[group_id, pair_id]]
        kernel_block = kernel_tile(owner_pts, partner_pts).astype(jnp.bfloat16)
        live_cols = (pair_id < pair_count[group_id]) & (jnp.arange(RMAX, dtype=jnp.int32) < pair_rank[group_id, pair_id])
        keep_mask = live_cols.astype(jnp.float32)
        row_part = jnp.dot(kernel_block, row_sketch[group_id, pair_id], preferred_element_type=jnp.float32) * keep_mask
        col_part = jnp.dot(kernel_block.T, col_sketch[group_id, pair_id], preferred_element_type=jnp.float32) * keep_mask
        return row_part.astype(jnp.bfloat16), col_part.astype(jnp.bfloat16)

    row_part, col_part = lax.map(one_pair, (group_grid.reshape(-1), pair_grid.reshape(-1)))
    row_factor = row_part.reshape(GROUPS, PAIRS, CLS, RMAX)
    col_factor = jnp.zeros((GROUPS, GROUPS, CAP, CLS, RMAX), jnp.bfloat16)
    col_factor = col_factor.at[pair_src.reshape(-1), group_grid.reshape(-1), slot_index.reshape(-1)].set(col_part)
    return row_factor, col_factor
```

```python
import functools

import jax
import jax.numpy as jnp
from jax import lax
from jax.experimental import pallas as pl
from jax.experimental.pallas import tpu as pltpu
from jax.sharding import PartitionSpec as P

CAP = 2
CHUNKS = 4
LOG2E = 1.4426950408889634
MESH = pl.DeviceIdType.MESH


def shift_order(ny, nz, nc):
    near = [(0, 1), (0, 3), (1, 0), (3, 0)]
    diagonal = [(1, 1), (3, 3), (1, 3), (3, 1)]
    far = [(2, 1), (2, 3), (1, 2), (3, 2)]
    straight = [(2, 0), (0, 2), (2, 2)]
    shifts = [(a, b, c) for a, b in straight + far + diagonal + near for c in range(nc)]
    return shifts + [(0, 0, c) for c in range(1, nc)]


def kernel(
    dims,
    idx,
    req,
    points,
    row_sketch,
    col_sketch,
    row_out,
    col_out,
    pts,
    rsk,
    csk,
    asked_v,
    asked_s,
    osend,
    left,
    lnorm,
    acc,
    rowv,
    *rest,
):
    groups, subs, own, strip, rank, chunks = dims
    rows = strip // chunks
    pairs = own * subs
    slots = groups * CAP
    send1, recv1, send2, right, col3, rcol, send4 = (
        rest[k * chunks : (k + 1) * chunks] for k in range(7)
    )
    (
        in_sem,
        out_sem,
        local_sem,
        idx_ssem,
        idx_rsem,
        own_ssem,
        own_rsem,
        far1_ssem,
        far1_rsem,
        x2_ssem,
        x2_rsem,
        x3_ssem,
        x3_rsem,
        far4_ssem,
        far4_rsem,
    ) = rest[7 * chunks :]
    me = lax.axis_index("clu")
    sub = lax.axis_index("sub")
    y, z, core = me // 8, lax.rem(me // 2, 4), lax.rem(me, 2)
    shifts = shift_order(4, 4, 2)
    peers = [
        (lax.rem(y + a, 4) * 4 + lax.rem(z + b, 4)) * 2 + lax.rem(core + c, 2) for a, b, c in shifts
    ]
    turns = [2, 1, 3]
    mates = [lax.rem(sub + k, subs) for k in turns]

    loads = [
        pltpu.make_async_copy(points, pts, in_sem.at[0]),
        pltpu.make_async_copy(row_sketch, rsk, in_sem.at[1]),
        pltpu.make_async_copy(col_sketch, csk, in_sem.at[2]),
    ]
    for copy in loads:
        copy.start()
    barrier = pltpu.get_barrier_semaphore()
    for peer in peers:
        pl.semaphore_signal(barrier, inc=1, device_id={"clu": peer}, device_id_type=MESH)
    for mate in mates:
        pl.semaphore_signal(barrier, inc=1, device_id={"sub": mate}, device_id_type=MESH)
    pl.semaphore_wait(barrier, len(peers) + len(mates))

    pending = []

    def send_clu(src, dst, ssem, rsem, peer):
        copy = pltpu.make_async_remote_copy(
            src_ref=src,
            dst_ref=dst,
            send_sem=ssem,
            recv_sem=rsem,
            device_id={"clu": peer},
            device_id_type=MESH,
        )
        copy.start()
        pending.append(copy)
        return copy

    def send_sub(src, dst, ssem, rsem, mate):
        copy = pltpu.make_async_remote_copy(
            src_ref=src,
            dst_ref=dst,
            send_sem=ssem,
            recv_sem=rsem,
            device_id={"sub": mate},
            device_id_type=MESH,
        )
        copy.start()
        pending.append(copy)
        return copy

    asks = [
        send_clu(req.at[peer], asked_v.at[me], idx_ssem.at[k], idx_rsem.at[k], peer)
        for k, peer in enumerate(peers)
    ]
    asked_v[me] = req[me]

    loads[0].wait()

    def pick_owner(p, carry):
        osend[p // own, lax.rem(p, own)] = pts[idx[pairs + p]]
        return carry

    lax.fori_loop(0, pairs, pick_owner, 0)
    owners = [
        send_sub(osend.at[mate], left.at[sub], own_ssem.at[k], own_rsem.at[k], mate)
        for k, mate in enumerate(mates)
    ]
    left[sub] = osend[sub]

    for copy in asks:
        copy.wait_recv()
    to_scalar = pltpu.make_async_copy(asked_v, asked_s, in_sem.at[3])
    to_scalar.start()
    to_scalar.wait()

    first = []
    for j in range(chunks):

        def pick(t, carry, j=j):
            g = t // CAP
            c = lax.rem(t, CAP)
            send1[j][t] = pts[asked_s[g, 0, c], pl.ds(j * rows, rows)]
            return carry

        lax.fori_loop(0, slots, pick, 0)
        first.append(
            [
                send_clu(
                    send1[j].at[pl.ds(peer * CAP, CAP)],
                    recv1[j].at[pl.ds(me * CAP, CAP)],
                    far1_ssem.at[j, k],
                    far1_rsem.at[j, k],
                    peer,
                )
                for k, peer in enumerate(peers)
            ]
        )
        recv1[j][pl.ds(me * CAP, CAP)] = send1[j][pl.ds(me * CAP, CAP)]
        rcol[j][pairs] = jnp.zeros((rows, rank), jnp.bfloat16)

    for copy in owners:
        copy.wait_recv()
    for copy in loads[1:]:
        copy.wait()

    def norms(i, carry):
        u = left[:, i].reshape(subs * strip, -1).astype(jnp.float32)
        lnorm[i] = lax.dot_general(
            jnp.ones((8, u.shape[1]), jnp.float32),
            u * u * (LOG2E / u.shape[1]),
            (((1,), (1,)), ((), ())),
            precision=lax.Precision.HIGHEST,
            preferred_element_type=jnp.float32,
        )
        return carry

    lax.fori_loop(0, own, norms, 0)

    def forward(j):
        for copy in first[j]:
            copy.wait_recv()

        def pick(p, carry):
            send2[j][p // own, lax.rem(p, own)] = recv1[j][idx[p]]
            return carry

        lax.fori_loop(0, pairs, pick, 0)
        copies = [
            send_sub(
                send2[j].at[mate], right[j].at[sub], x2_ssem.at[j, k], x2_rsem.at[j, k], mate
            )
            for k, mate in enumerate(mates)
        ]
        right[j][sub] = send2[j][sub]
        return copies

    def compute(j, copies):
        for copy in copies:
            copy.wait_recv()

        def one(i, carry):
            u = left[:, i].reshape(subs * strip, -1)
            v = right[j][:, i].reshape(subs * rows, -1)
            width = u.shape[1]
            inner = lax.dot_general(
                v, u, (((1,), (1,)), ((), ())), preferred_element_type=jnp.float32
            )
            wide = v.astype(jnp.float32)
            vnorm = jnp.sum(wide * wide, axis=1, keepdims=True) * (LOG2E / width)
            tile = jnp.exp2(inner * (2.0 * LOG2E / width) - lnorm[i][0:1] - vnorm)
            tile = tile.astype(jnp.bfloat16)
            live = idx[2 * pairs + sub * own + i]
            keep = (lax.broadcasted_iota(jnp.int32, (1, rank), 1) < live).astype(jnp.float32)
            col = jnp.dot(tile, csk[i], preferred_element_type=jnp.float32) * keep
            col3[j][:, i] = col.astype(jnp.bfloat16).reshape(subs, rows, rank)
            side = rsk[i].reshape(subs, strip, rank)[:, j * rows : (j + 1) * rows]
            part = lax.dot_general(
                tile,
                side.reshape(subs * rows, rank),
                (((0,), (0,)), ((), ())),
                preferred_element_type=jnp.float32,
            )
            if j == 0:
                acc[i] = part
            elif j < chunks - 1:
                acc[i] += part
            else:
                rowv[i] = ((acc[i] + part) * keep).astype(jnp.bfloat16)
            return carry

        lax.fori_loop(0, own, one, 0)
        outgoing = [
            send_sub(
                col3[j].at[mate],
                rcol[j].at[pl.ds(sub * own, own)],
                x3_ssem.at[j, k],
                x3_rsem.at[j, k],
                mate,
            )
            for k, mate in enumerate(mates)
        ]
        rcol[j][pl.ds(sub * own, own)] = col3[j][sub]
        return outgoing

    landed = []

    def give_back(j, copies):
        for copy in copies:
            copy.wait_recv()

        def pick(t, carry):
            send4[j][t // CAP, lax.rem(t, CAP)] = rcol[j][idx[3 * pairs + t]]
            return carry

        lax.fori_loop(0, slots, pick, 0)
        place = pl.ds(j * rows, rows)
        for k, peer in enumerate(peers):
            landed.append(
                send_clu(
                    send4[j].at[peer],
                    col_out.at[me, :, place],
                    far4_ssem.at[j, k],
                    far4_rsem.at[j, k],
                    peer,
                )
            )
        mine = pltpu.make_async_copy(send4[j].at[me], col_out.at[me, :, place], local_sem.at[j])
        mine.start()
        return mine

    local = []
    back = None
    for j in range(chunks):
        moved = forward(j)
        if back is not None:
            local.append(give_back(j - 1, back))
        back = compute(j, moved)
    store = pltpu.make_async_copy(rowv, row_out, out_sem)
    store.start()
    local.append(give_back(chunks - 1, back))

    for copy in pending:
        copy.wait_send()
    for copy in landed:
        copy.wait_recv()
    for copy in local:
        copy.wait()
    store.wait()


def shards(
    points, row_sketch, col_sketch, pair_count, pair_local, pair_src, pair_partner, pair_rank
):
    groups = lax.axis_size("clu")
    subs = lax.axis_size("sub")
    clusters, strip, width = points.shape
    pairs = pair_src.shape[1]
    own = pairs // subs
    rank = row_sketch.shape[3]
    chunks = CHUNKS
    rows = strip // chunks
    slots = groups * CAP

    sources = pair_src[0]
    position = jnp.arange(pairs, dtype=jnp.int32)
    earlier = (sources[:, None] == sources[None, :]) & (position[None, :] < position[:, None])
    target = sources * CAP + jnp.sum(earlier.astype(jnp.int32), axis=1)
    hits = target[None, :] == jnp.arange(slots, dtype=jnp.int32)[:, None]
    code = jnp.sum(jnp.where(hits, position * clusters + pair_partner[0] - pairs * clusters, 0), axis=1)
    code = code + pairs * clusters
    named = code // clusters
    wanted = lax.rem(code, clusters)
    live = jnp.where(position < pair_count[0], pair_rank[0], 0)
    idx = jnp.concatenate([target, pair_local[0], live, named])
    req = jnp.pad(wanted.reshape(groups, 1, CAP), ((0, 0), (0, 0), (0, 128 - CAP)))

    per_chunk = [
        ((slots, rows, width), jnp.bfloat16),
        ((slots, rows, width), jnp.bfloat16),
        ((subs, own, rows, width), jnp.bfloat16),
        ((subs, own, rows, width), jnp.bfloat16),
        ((subs, own, rows, rank), jnp.bfloat16),
        ((pairs + 1, rows, rank), jnp.bfloat16),
        ((groups, CAP, rows, rank), jnp.bfloat16),
    ]
    scratch = [
        pltpu.VMEM((clusters, strip, width), jnp.bfloat16),
        pltpu.VMEM((own, subs * strip, rank), jnp.bfloat16),
        pltpu.VMEM((own, subs * strip, rank), jnp.bfloat16),
        pltpu.VMEM((groups, 1, 128), jnp.int32),
        pltpu.SMEM((groups, 1, 128), jnp.int32),
        pltpu.VMEM((subs, own, strip, width), jnp.bfloat16),
        pltpu.VMEM((subs, own, strip, width), jnp.bfloat16),
        pltpu.VMEM((own, 8, subs * strip), jnp.float32),
        pltpu.VMEM((own, subs * strip, rank), jnp.float32),
        pltpu.VMEM((own, subs * strip, rank), jnp.bfloat16),
    ]
    for shape, dtype in per_chunk:
        scratch += [pltpu.VMEM(shape, dtype) for _ in range(chunks)]
    dma = pltpu.SemaphoreType.DMA
    scratch += [
        dma((4,)),
        dma,
        dma((chunks,)),
        dma((groups - 1,)),
        dma((groups - 1,)),
        dma((subs - 1,)),
        dma((subs - 1,)),
        dma((chunks, groups - 1)),
        dma((chunks, groups - 1)),
        dma((chunks, subs - 1)),
        dma((chunks, subs - 1)),
        dma((chunks, subs - 1)),
        dma((chunks, subs - 1)),
        dma((chunks, groups - 1)),
        dma((chunks, groups - 1)),
    ]
    anywhere = pl.BlockSpec(memory_space=pl.ANY)
    row, col = pl.pallas_call(
        functools.partial(kernel, (groups, subs, own, strip, rank, chunks)),
        out_shape=(
            jax.ShapeDtypeStruct((own, subs * strip, rank), jnp.bfloat16),
            jax.ShapeDtypeStruct((groups, CAP, strip, rank), jnp.bfloat16),
        ),
        in_specs=[
            pl.BlockSpec(memory_space=pltpu.SMEM),
            pl.BlockSpec(memory_space=pltpu.VMEM),
            anywhere,
            anywhere,
            anywhere,
        ],
        out_specs=(anywhere, anywhere),
        scratch_shapes=scratch,
        compiler_params=pltpu.CompilerParams(
            collective_id=0, has_side_effects=True, vmem_limit_bytes=56 << 20
        ),
        name="pair_sketches",
    )(idx, req, points, row_sketch[0], col_sketch[0])
    return row[None], col[None]


def solution(mesh):
    placed = (
        P("clu", "sub", None),
        P("clu", "sub", None, None),
        P("clu", "sub", None, None),
        P("clu"),
        P("clu", None),
        P("clu", None),
        P("clu", None),
        P("clu", None),
    )
    return jax.shard_map(
        shards,
        mesh=mesh,
        in_specs=placed,
        out_specs=(P("clu", "sub", None, None), P("clu", None, None, "sub", None)),
        check_vma=False,
    )
```

```python
import functools

import jax
import jax.numpy as jnp
from jax import lax
from jax.experimental import pallas as pl
from jax.experimental.pallas import tpu as pltpu
from jax.sharding import PartitionSpec as P

CAP = 2
CHUNKS = 4
LOG2E = 1.4426950408889634
MESH = pl.DeviceIdType.MESH


def shift_order(ny, nz, nc):
    near = [(0, 1), (0, 3), (1, 0), (3, 0)]
    diagonal = [(1, 1), (3, 3), (1, 3), (3, 1)]
    far = [(2, 1), (2, 3), (1, 2), (3, 2)]
    straight = [(2, 0), (0, 2), (2, 2)]
    shifts = [(a, b, c) for c in range(nc) for a, b in straight + far + diagonal + near]
    return shifts + [(0, 0, c) for c in range(1, nc)]


def index_tables(count, source, place_of, partner, ranks, table, req):
    n = source.shape[1]
    down = lax.broadcasted_iota(jnp.int32, (n, n), 0)
    along = lax.broadcasted_iota(jnp.int32, (n, n), 1)

    def upright(row):
        return jnp.sum(jnp.where(down == along, row, 0), axis=1, keepdims=True)

    row = source[...]
    column = upright(row)
    same = column == row
    target = row * CAP + jnp.sum(jnp.where(same & (down < along), 1, 0), axis=0, keepdims=True)
    upright_target = column * CAP + jnp.sum(
        jnp.where(same & (along < down), 1, 0), axis=1, keepdims=True
    )
    hits = upright_target == lax.broadcasted_iota(jnp.int32, (n, 128), 1)
    pair = lax.broadcasted_iota(jnp.int32, (n, 128), 0)
    position = lax.broadcasted_iota(jnp.int32, (1, n), 1)
    table[...] = jnp.zeros_like(table)
    table[0, :, 0:n] = target
    table[1, :, 0:n] = place_of[...]
    table[2, :, 0:n] = jnp.where(position < count[0], ranks[...], 0)
    table[3] = jnp.sum(jnp.where(hits, pair - n, 0), axis=0, keepdims=True) + n
    req[...] = jnp.sum(jnp.where(hits, upright(partner[...]), 0), axis=0, keepdims=True)


def kernel(
    dims,
    count,
    source,
    place_of,
    partner,
    ranks,
    points,
    row_sketch,
    col_sketch,
    row_out,
    col_out,
    pts,
    rsk,
    csk,
    table,
    idx,
    req,
    asked_v,
    asked_s,
    osend,
    left,
    lnorm,
    acc,
    rowv,
    *rest,
):
    groups, subs, own, strip, rank, chunks = dims
    rows = strip // chunks
    pairs = own * subs
    slots = groups * CAP
    send1, recv1, send2, right, col3, rcol, send4 = (
        rest[k * chunks : (k + 1) * chunks] for k in range(7)
    )
    (
        in_sem,
        out_sem,
        local_sem,
        idx_ssem,
        idx_rsem,
        own_ssem,
        own_rsem,
        far1_ssem,
        far1_rsem,
        x2_ssem,
        x2_rsem,
        x3_ssem,
        x3_rsem,
        far4_ssem,
        far4_rsem,
    ) = rest[7 * chunks :]
    me = lax.axis_index("clu")
    sub = lax.axis_index("sub")
    y, z, core = me // 8, lax.rem(me // 2, 4), lax.rem(me, 2)
    shifts = shift_order(4, 4, 2)
    peers = [
        (lax.rem(y + a, 4) * 4 + lax.rem(z + b, 4)) * 2 + lax.rem(core + c, 2) for a, b, c in shifts
    ]
    turns = [2, 1, 3]
    mates = [lax.rem(sub + k, subs) for k in turns]

    loads = [
        pltpu.make_async_copy(points, pts, in_sem.at[0]),
        pltpu.make_async_copy(row_sketch, rsk, in_sem.at[1]),
        pltpu.make_async_copy(col_sketch, csk, in_sem.at[2]),
    ]
    for copy in loads:
        copy.start()
    barrier = pltpu.get_barrier_semaphore()
    for peer in peers:
        pl.semaphore_signal(barrier, inc=1, device_id={"clu": peer}, device_id_type=MESH)
    for mate in mates:
        pl.semaphore_signal(barrier, inc=1, device_id={"sub": mate}, device_id_type=MESH)
    index_tables(count, source, place_of, partner, ranks, table, req)
    to_scalar = pltpu.make_async_copy(table, idx, in_sem.at[3])
    to_scalar.start()
    pl.semaphore_wait(barrier, len(peers) + len(mates))

    pending = []

    def send_clu(src, dst, ssem, rsem, peer):
        copy = pltpu.make_async_remote_copy(
            src_ref=src,
            dst_ref=dst,
            send_sem=ssem,
            recv_sem=rsem,
            device_id={"clu": peer},
            device_id_type=MESH,
        )
        copy.start()
        pending.append(copy)
        return copy

    def send_sub(src, dst, ssem, rsem, mate):
        copy = pltpu.make_async_remote_copy(
            src_ref=src,
            dst_ref=dst,
            send_sem=ssem,
            recv_sem=rsem,
            device_id={"sub": mate},
            device_id_type=MESH,
        )
        copy.start()
        pending.append(copy)
        return copy

    asks = [
        send_clu(req, asked_v.at[me], idx_ssem.at[k], idx_rsem.at[k], peer)
        for k, peer in enumerate(peers)
    ]
    asked_v[me] = req[...]
    to_scalar.wait()

    loads[0].wait()

    def pick_owner(p, carry):
        osend[p // own, lax.rem(p, own)] = pts[idx[1, 0, p]]
        return carry

    lax.fori_loop(0, pairs, pick_owner, 0)
    owners = [
        send_sub(osend.at[mate], left.at[sub], own_ssem.at[k], own_rsem.at[k], mate)
        for k, mate in enumerate(mates)
    ]
    left[sub] = osend[sub]

    for copy in asks:
        copy.wait_recv()
    to_scalar = pltpu.make_async_copy(asked_v, asked_s, in_sem.at[4])
    to_scalar.start()
    to_scalar.wait()

    first, moved, back, landed, local = {}, {}, {}, [], []

    def launch(j):
        def pick(t, carry):
            wanted = asked_s[t // CAP, 0, me * CAP + lax.rem(t, CAP)]
            send1[j][t] = pts[wanted, pl.ds(j * rows, rows)]
            return carry

        lax.fori_loop(0, slots, pick, 0)
        first[j] = [
            send_clu(
                send1[j].at[pl.ds(peer * CAP, CAP)],
                recv1[j].at[pl.ds(me * CAP, CAP)],
                far1_ssem.at[j, k],
                far1_rsem.at[j, k],
                peer,
            )
            for k, peer in enumerate(peers)
        ]
        recv1[j][pl.ds(me * CAP, CAP)] = send1[j][pl.ds(me * CAP, CAP)]
        rcol[j][pairs] = jnp.zeros((rows, rank), jnp.bfloat16)

    def norms():
        for copy in owners:
            copy.wait_recv()
        for copy in loads[1:]:
            copy.wait()

        def norms_of(i, carry):
            u = left[:, i].reshape(subs * strip, -1).astype(jnp.float32)
            lnorm[i] = lax.dot_general(
                jnp.ones((8, u.shape[1]), jnp.float32),
                u * u * (LOG2E / u.shape[1]),
                (((1,), (1,)), ((), ())),
                precision=lax.Precision.HIGHEST,
                preferred_element_type=jnp.float32,
            )
            return carry

        lax.fori_loop(0, own, norms_of, 0)

    def forward(j):
        for copy in first[j]:
            copy.wait_recv()

        def pick(p, carry):
            send2[j][p // own, lax.rem(p, own)] = recv1[j][idx[0, 0, p]]
            return carry

        lax.fori_loop(0, pairs, pick, 0)
        moved[j] = [
            send_sub(
                send2[j].at[mate], right[j].at[sub], x2_ssem.at[j, k], x2_rsem.at[j, k], mate
            )
            for k, mate in enumerate(mates)
        ]
        right[j][sub] = send2[j][sub]

    def compute(j):
        for copy in moved[j]:
            copy.wait_recv()

        def one(i, carry):
            u = left[:, i].reshape(subs * strip, -1)
            v = right[j][:, i].reshape(subs * rows, -1)
            width = u.shape[1]
            inner = lax.dot_general(
                v, u, (((1,), (1,)), ((), ())), preferred_element_type=jnp.float32
            )
            wide = v.astype(jnp.float32)
            vnorm = jnp.sum(wide * wide, axis=1, keepdims=True) * (LOG2E / width)
            tile = jnp.exp2(inner * (2.0 * LOG2E / width) - lnorm[i][0:1] - vnorm)
            tile = tile.astype(jnp.bfloat16)
            live = idx[2, 0, sub * own + i]
            keep = (lax.broadcasted_iota(jnp.int32, (1, rank), 1) < live).astype(jnp.float32)
            col = jnp.dot(tile, csk[i], preferred_element_type=jnp.float32) * keep
            col3[j][:, i] = col.astype(jnp.bfloat16).reshape(subs, rows, rank)
            side = rsk[i].reshape(subs, strip, rank)[:, j * rows : (j + 1) * rows]
            part = lax.dot_general(
                tile,
                side.reshape(subs * rows, rank),
                (((0,), (0,)), ((), ())),
                preferred_element_type=jnp.float32,
            )
            if j == 0:
                acc[i] = part
            elif j < chunks - 1:
                acc[i] += part
            else:
                rowv[i] = ((acc[i] + part) * keep).astype(jnp.bfloat16)
            return carry

        lax.fori_loop(0, own, one, 0)
        back[j] = [
            send_sub(
                col3[j].at[mate],
                rcol[j].at[pl.ds(sub * own, own)],
                x3_ssem.at[j, k],
                x3_rsem.at[j, k],
                mate,
            )
            for k, mate in enumerate(mates)
        ]
        rcol[j][pl.ds(sub * own, own)] = col3[j][sub]

    def give_back(j):
        for copy in back[j]:
            copy.wait_recv()

        def pick(t, carry):
            send4[j][t // CAP, lax.rem(t, CAP)] = rcol[j][idx[3, 0, t]]
            return carry

        lax.fori_loop(0, slots, pick, 0)
        place = pl.ds(j * rows, rows)
        for k, peer in enumerate(peers):
            landed.append(
                send_clu(
                    send4[j].at[peer],
                    col_out.at[me, :, place],
                    far4_ssem.at[j, k],
                    far4_rsem.at[j, k],
                    peer,
                )
            )
        mine = pltpu.make_async_copy(send4[j].at[me], col_out.at[me, :, place], local_sem.at[j])
        mine.start()
        local.append(mine)

    for j in range(chunks):
        launch(j)
    norms()
    forward(0)
    for j in range(chunks):
        if j + 1 < chunks:
            forward(j + 1)
        compute(j)
        if j > 0:
            give_back(j - 1)
    store = pltpu.make_async_copy(rowv, row_out, out_sem)
    store.start()
    give_back(chunks - 1)

    for copy in pending:
        copy.wait_send()
    for copy in landed:
        copy.wait_recv()
    for copy in local:
        copy.wait()
    store.wait()


def shards(
    points, row_sketch, col_sketch, pair_count, pair_local, pair_src, pair_partner, pair_rank
):
    groups = lax.axis_size("clu")
    subs = lax.axis_size("sub")
    clusters, strip, width = points.shape
    pairs = pair_src.shape[1]
    own = pairs // subs
    rank = row_sketch.shape[3]
    chunks = CHUNKS
    rows = strip // chunks
    slots = groups * CAP

    per_chunk = [
        ((slots, rows, width), jnp.bfloat16),
        ((slots, rows, width), jnp.bfloat16),
        ((subs, own, rows, width), jnp.bfloat16),
        ((subs, own, rows, width), jnp.bfloat16),
        ((subs, own, rows, rank), jnp.bfloat16),
        ((pairs + 1, rows, rank), jnp.bfloat16),
        ((groups, CAP, rows, rank), jnp.bfloat16),
    ]
    scratch = [
        pltpu.VMEM((clusters, strip, width), jnp.bfloat16),
        pltpu.VMEM((own, subs * strip, rank), jnp.bfloat16),
        pltpu.VMEM((own, subs * strip, rank), jnp.bfloat16),
        pltpu.VMEM((4, 1, 128), jnp.int32),
        pltpu.SMEM((4, 1, 128), jnp.int32),
        pltpu.VMEM((1, 128), jnp.int32),
        pltpu.VMEM((groups, 1, 128), jnp.int32),
        pltpu.SMEM((groups, 1, 128), jnp.int32),
        pltpu.VMEM((subs, own, strip, width), jnp.bfloat16),
        pltpu.VMEM((subs, own, strip, width), jnp.bfloat16),
        pltpu.VMEM((own, 8, subs * strip), jnp.float32),
        pltpu.VMEM((own, subs * strip, rank), jnp.float32),
        pltpu.VMEM((own, subs * strip, rank), jnp.bfloat16),
    ]
    for shape, dtype in per_chunk:
        scratch += [pltpu.VMEM(shape, dtype) for _ in range(chunks)]
    dma = pltpu.SemaphoreType.DMA
    scratch += [
        dma((5,)),
        dma,
        dma((chunks,)),
        dma((groups - 1,)),
        dma((groups - 1,)),
        dma((subs - 1,)),
        dma((subs - 1,)),
        dma((chunks, groups - 1)),
        dma((chunks, groups - 1)),
        dma((chunks, subs - 1)),
        dma((chunks, subs - 1)),
        dma((chunks, subs - 1)),
        dma((chunks, subs - 1)),
        dma((chunks, groups - 1)),
        dma((chunks, groups - 1)),
    ]
    small = pl.BlockSpec(memory_space=pltpu.VMEM)
    anywhere = pl.BlockSpec(memory_space=pl.ANY)
    row, col = pl.pallas_call(
        functools.partial(kernel, (groups, subs, own, strip, rank, chunks)),
        out_shape=(
            jax.ShapeDtypeStruct((own, subs * strip, rank), jnp.bfloat16),
            jax.ShapeDtypeStruct((groups, CAP, strip, rank), jnp.bfloat16),
        ),
        in_specs=[
            pl.BlockSpec(memory_space=pltpu.SMEM),
            small,
            small,
            small,
            small,
            anywhere,
            anywhere,
            anywhere,
        ],
        out_specs=(anywhere, anywhere),
        scratch_shapes=scratch,
        compiler_params=pltpu.CompilerParams(
            collective_id=0, has_side_effects=True, vmem_limit_bytes=56 << 20
        ),
        name="pair_sketches",
    )(
        pair_count,
        pair_src,
        pair_local,
        pair_partner,
        pair_rank,
        points,
        row_sketch[0],
        col_sketch[0],
    )
    return row[None], col[None]


def solution(mesh):
    placed = (
        P("clu", "sub", None),
        P("clu", "sub", None, None),
        P("clu", "sub", None, None),
        P("clu"),
        P("clu", None),
        P("clu", None),
        P("clu", None),
        P("clu", None),
    )
    return jax.shard_map(
        shards,
        mesh=mesh,
        in_specs=placed,
        out_specs=(P("clu", "sub", None, None), P("clu", None, None, "sub", None)),
        check_vma=False,
    )
```

```python
import functools

import jax
import jax.numpy as jnp
from jax import lax
from jax.experimental import pallas as pl
from jax.experimental.pallas import tpu as pltpu
from jax.sharding import PartitionSpec as P

CAP = 2
CHUNKS = 4
LOG2E = 1.4426950408889634
MESH = pl.DeviceIdType.MESH


def shift_order(ny, nz, nc):
    near = [(0, 1), (0, 3), (1, 0), (3, 0)]
    diagonal = [(1, 1), (3, 3), (1, 3), (3, 1)]
    far = [(2, 1), (2, 3), (1, 2), (3, 2)]
    straight = [(2, 0), (0, 2), (2, 2)]
    shifts = [(a, b, c) for c in range(nc) for a, b in straight + far + diagonal + near]
    return shifts + [(0, 0, c) for c in range(1, nc)]


def index_tables(count, source, place_of, partner, ranks, table, req):
    n = source.shape[1]
    down = lax.broadcasted_iota(jnp.int32, (n, n), 0)
    along = lax.broadcasted_iota(jnp.int32, (n, n), 1)

    def upright(row):
        return jnp.sum(jnp.where(down == along, row, 0), axis=1, keepdims=True)

    row = source[...]
    column = upright(row)
    same = column == row
    target = row * CAP + jnp.sum(jnp.where(same & (down < along), 1, 0), axis=0, keepdims=True)
    upright_target = column * CAP + jnp.sum(
        jnp.where(same & (along < down), 1, 0), axis=1, keepdims=True
    )
    hits = upright_target == lax.broadcasted_iota(jnp.int32, (n, 128), 1)
    pair = lax.broadcasted_iota(jnp.int32, (n, 128), 0)
    position = lax.broadcasted_iota(jnp.int32, (1, n), 1)
    table[...] = jnp.zeros_like(table)
    table[0, :, 0:n] = target
    table[1, :, 0:n] = place_of[...]
    table[2, :, 0:n] = jnp.where(position < count[0], ranks[...], 0)
    table[3] = jnp.sum(jnp.where(hits, pair - n, 0), axis=0, keepdims=True) + n
    req[...] = jnp.sum(jnp.where(hits, upright(partner[...]), 0), axis=0, keepdims=True)


def kernel(
    dims,
    count,
    source,
    place_of,
    partner,
    ranks,
    points,
    row_sketch,
    col_sketch,
    row_out,
    col_out,
    pts,
    rsk,
    csk,
    table,
    idx,
    req,
    asked_v,
    asked_s,
    osend,
    left,
    lnorm,
    acc,
    rowv,
    *rest,
):
    groups, subs, own, strip, rank, chunks = dims
    rows = strip // chunks
    pairs = own * subs
    slots = groups * CAP
    send1, recv1, send2, right, col3, rcol, send4 = (
        rest[k * chunks : (k + 1) * chunks] for k in range(7)
    )
    (
        in_sem,
        out_sem,
        local_sem,
        idx_ssem,
        idx_rsem,
        own_ssem,
        own_rsem,
        far1_ssem,
        far1_rsem,
        x2_ssem,
        x2_rsem,
        x3_ssem,
        x3_rsem,
        far4_ssem,
        far4_rsem,
    ) = rest[7 * chunks :]
    me = lax.axis_index("clu")
    sub = lax.axis_index("sub")
    y, z, core = me // 8, lax.rem(me // 2, 4), lax.rem(me, 2)
    shifts = shift_order(4, 4, 2)
    peers = [
        (lax.rem(y + a, 4) * 4 + lax.rem(z + b, 4)) * 2 + lax.rem(core + c, 2) for a, b, c in shifts
    ]
    turns = [2, 1, 3]
    mates = [lax.rem(sub + k, subs) for k in turns]

    loads = [
        pltpu.make_async_copy(points, pts, in_sem.at[0]),
        pltpu.make_async_copy(row_sketch, rsk, in_sem.at[1]),
        pltpu.make_async_copy(col_sketch, csk, in_sem.at[2]),
    ]
    for copy in loads:
        copy.start()
    barrier = pltpu.get_barrier_semaphore()
    for peer in peers:
        pl.semaphore_signal(barrier, inc=1, device_id={"clu": peer}, device_id_type=MESH)
    for mate in mates:
        pl.semaphore_signal(barrier, inc=1, device_id={"sub": mate}, device_id_type=MESH)
    index_tables(count, source, place_of, partner, ranks, table, req)
    to_scalar = pltpu.make_async_copy(table, idx, in_sem.at[3])
    to_scalar.start()
    to_scalar.wait()
    loads[0].wait()

    def pick_owner(p, carry):
        osend[p // own, lax.rem(p, own)] = pts[idx[1, 0, p]]
        return carry

    lax.fori_loop(0, pairs, pick_owner, 0)
    pl.semaphore_wait(barrier, len(peers) + len(mates))

    def send(src, dst, ssem, rsem, axis, to):
        pltpu.make_async_remote_copy(
            src_ref=src,
            dst_ref=dst,
            send_sem=ssem,
            recv_sem=rsem,
            device_id={axis: to},
            device_id_type=MESH,
        ).start()

    def await_all(ref, count, sem):
        blocks = ref.at[pl.ds(0, count)]
        pltpu.make_async_copy(blocks, blocks, sem).wait()

    for peer in peers:
        send(req, asked_v.at[me], idx_ssem, idx_rsem, "clu", peer)
    asked_v[me] = req[...]

    for mate in mates:
        send(osend.at[mate], left.at[sub], own_ssem, own_rsem, "sub", mate)
    left[sub] = osend[sub]

    await_all(asked_v, groups - 1, idx_rsem)
    to_scalar = pltpu.make_async_copy(asked_v, asked_s, in_sem.at[4])
    to_scalar.start()
    to_scalar.wait()

    local = []

    def launch(j):
        def pick(t, carry):
            wanted = asked_s[t // CAP, 0, me * CAP + lax.rem(t, CAP)]
            send1[j][t] = pts[wanted, pl.ds(j * rows, rows)]
            return carry

        lax.fori_loop(0, slots, pick, 0)
        for peer in peers:
            send(
                send1[j].at[pl.ds(peer * CAP, CAP)],
                recv1[j].at[pl.ds(me * CAP, CAP)],
                far1_ssem.at[j],
                far1_rsem.at[j],
                "clu",
                peer,
            )
        recv1[j][pl.ds(me * CAP, CAP)] = send1[j][pl.ds(me * CAP, CAP)]
        rcol[j][pairs] = jnp.zeros((rows, rank), jnp.bfloat16)

    def norms():
        await_all(left, subs - 1, own_rsem)
        for copy in loads[1:]:
            copy.wait()

        def norms_of(i, carry):
            u = left[:, i].reshape(subs * strip, -1).astype(jnp.float32)
            lnorm[i] = lax.dot_general(
                jnp.ones((8, u.shape[1]), jnp.float32),
                u * u * (LOG2E / u.shape[1]),
                (((1,), (1,)), ((), ())),
                precision=lax.Precision.HIGHEST,
                preferred_element_type=jnp.float32,
            )
            return carry

        lax.fori_loop(0, own, norms_of, 0)

    def forward(j):
        await_all(recv1[j], slots - CAP, far1_rsem.at[j])

        def pick(p, carry):
            send2[j][p // own, lax.rem(p, own)] = recv1[j][idx[0, 0, p]]
            return carry

        lax.fori_loop(0, pairs, pick, 0)
        for mate in mates:
            send(send2[j].at[mate], right[j].at[sub], x2_ssem.at[j], x2_rsem.at[j], "sub", mate)
        right[j][sub] = send2[j][sub]

    def compute(j):
        await_all(right[j], subs - 1, x2_rsem.at[j])

        def one(i, carry):
            u = left[:, i].reshape(subs * strip, -1)
            v = right[j][:, i].reshape(subs * rows, -1)
            width = u.shape[1]
            inner = lax.dot_general(
                v, u, (((1,), (1,)), ((), ())), preferred_element_type=jnp.float32
            )
            wide = v.astype(jnp.float32)
            vnorm = jnp.sum(wide * wide, axis=1, keepdims=True) * (LOG2E / width)
            tile = jnp.exp2(inner * (2.0 * LOG2E / width) - lnorm[i][0:1] - vnorm)
            tile = tile.astype(jnp.bfloat16)
            live = idx[2, 0, sub * own + i]
            keep = (lax.broadcasted_iota(jnp.int32, (1, rank), 1) < live).astype(jnp.float32)
            col = jnp.dot(tile, csk[i], preferred_element_type=jnp.float32) * keep
            col3[j][:, i] = col.astype(jnp.bfloat16).reshape(subs, rows, rank)
            side = rsk[i].reshape(subs, strip, rank)[:, j * rows : (j + 1) * rows]
            part = lax.dot_general(
                tile,
                side.reshape(subs * rows, rank),
                (((0,), (0,)), ((), ())),
                preferred_element_type=jnp.float32,
            )
            if j == 0:
                acc[i] = part
            elif j < chunks - 1:
                acc[i] += part
            else:
                rowv[i] = ((acc[i] + part) * keep).astype(jnp.bfloat16)
            return carry

        lax.fori_loop(0, own, one, 0)
        for mate in mates:
            send(
                col3[j].at[mate],
                rcol[j].at[pl.ds(sub * own, own)],
                x3_ssem.at[j],
                x3_rsem.at[j],
                "sub",
                mate,
            )
        rcol[j][pl.ds(sub * own, own)] = col3[j][sub]

    def give_back(j):
        await_all(rcol[j], pairs - own, x3_rsem.at[j])

        def pick(t, carry):
            send4[j][t // CAP, lax.rem(t, CAP)] = rcol[j][idx[3, 0, t]]
            return carry

        lax.fori_loop(0, slots, pick, 0)
        place = pl.ds(j * rows, rows)
        for peer in peers:
            send(
                send4[j].at[peer],
                col_out.at[me, :, place],
                far4_ssem.at[j],
                far4_rsem,
                "clu",
                peer,
            )
        mine = pltpu.make_async_copy(send4[j].at[me], col_out.at[me, :, place], local_sem.at[j])
        mine.start()
        local.append(mine)

    for j in range(chunks):
        launch(j)
    norms()
    forward(0)
    for j in range(chunks):
        if j + 1 < chunks:
            forward(j + 1)
        compute(j)
        if j > 0:
            give_back(j - 1)
    store = pltpu.make_async_copy(rowv, row_out, out_sem)
    store.start()
    give_back(chunks - 1)

    await_all(asked_v, groups - 1, idx_ssem)
    await_all(left, subs - 1, own_ssem)
    for j in range(chunks):
        await_all(send1[j], slots - CAP, far1_ssem.at[j])
        await_all(send2[j], subs - 1, x2_ssem.at[j])
        await_all(col3[j], subs - 1, x3_ssem.at[j])
        await_all(send4[j], groups - 1, far4_ssem.at[j])
    await_all(col_out, groups - 1, far4_rsem)
    for copy in local:
        copy.wait()
    store.wait()


def shards(
    points, row_sketch, col_sketch, pair_count, pair_local, pair_src, pair_partner, pair_rank
):
    groups = lax.axis_size("clu")
    subs = lax.axis_size("sub")
    clusters, strip, width = points.shape
    pairs = pair_src.shape[1]
    own = pairs // subs
    rank = row_sketch.shape[3]
    chunks = CHUNKS
    rows = strip // chunks
    slots = groups * CAP

    per_chunk = [
        ((slots, rows, width), jnp.bfloat16),
        ((slots, rows, width), jnp.bfloat16),
        ((subs, own, rows, width), jnp.bfloat16),
        ((subs, own, rows, width), jnp.bfloat16),
        ((subs, own, rows, rank), jnp.bfloat16),
        ((pairs + 1, rows, rank), jnp.bfloat16),
        ((groups, CAP, rows, rank), jnp.bfloat16),
    ]
    scratch = [
        pltpu.VMEM((clusters, strip, width), jnp.bfloat16),
        pltpu.VMEM((own, subs * strip, rank), jnp.bfloat16),
        pltpu.VMEM((own, subs * strip, rank), jnp.bfloat16),
        pltpu.VMEM((4, 1, 128), jnp.int32),
        pltpu.SMEM((4, 1, 128), jnp.int32),
        pltpu.VMEM((1, 128), jnp.int32),
        pltpu.VMEM((groups, 1, 128), jnp.int32),
        pltpu.SMEM((groups, 1, 128), jnp.int32),
        pltpu.VMEM((subs, own, strip, width), jnp.bfloat16),
        pltpu.VMEM((subs, own, strip, width), jnp.bfloat16),
        pltpu.VMEM((own, 8, subs * strip), jnp.float32),
        pltpu.VMEM((own, subs * strip, rank), jnp.float32),
        pltpu.VMEM((own, subs * strip, rank), jnp.bfloat16),
    ]
    for shape, dtype in per_chunk:
        scratch += [pltpu.VMEM(shape, dtype) for _ in range(chunks)]
    dma = pltpu.SemaphoreType.DMA
    scratch += [
        dma((5,)),
        dma,
        dma((chunks,)),
        dma,
        dma,
        dma,
        dma,
        dma((chunks,)),
        dma((chunks,)),
        dma((chunks,)),
        dma((chunks,)),
        dma((chunks,)),
        dma((chunks,)),
        dma((chunks,)),
        dma,
    ]
    small = pl.BlockSpec(memory_space=pltpu.VMEM)
    anywhere = pl.BlockSpec(memory_space=pl.ANY)
    row, col = pl.pallas_call(
        functools.partial(kernel, (groups, subs, own, strip, rank, chunks)),
        out_shape=(
            jax.ShapeDtypeStruct((own, subs * strip, rank), jnp.bfloat16),
            jax.ShapeDtypeStruct((groups, CAP, strip, rank), jnp.bfloat16),
        ),
        in_specs=[
            pl.BlockSpec(memory_space=pltpu.SMEM),
            small,
            small,
            small,
            small,
            anywhere,
            anywhere,
            anywhere,
        ],
        out_specs=(anywhere, anywhere),
        scratch_shapes=scratch,
        compiler_params=pltpu.CompilerParams(
            collective_id=0, has_side_effects=True, vmem_limit_bytes=56 << 20
        ),
        name="pair_sketches",
    )(
        pair_count,
        pair_src,
        pair_local,
        pair_partner,
        pair_rank,
        points,
        row_sketch[0],
        col_sketch[0],
    )
    return row[None], col[None]


def solution(mesh):
    placed = (
        P("clu", "sub", None),
        P("clu", "sub", None, None),
        P("clu", "sub", None, None),
        P("clu"),
        P("clu", None),
        P("clu", None),
        P("clu", None),
        P("clu", None),
    )
    return jax.shard_map(
        shards,
        mesh=mesh,
        in_specs=placed,
        out_specs=(P("clu", "sub", None, None), P("clu", None, None, "sub", None)),
        check_vma=False,
    )
```

```python
import functools

import jax
import jax.numpy as jnp
from jax import lax
from jax.experimental import pallas as pl
from jax.experimental.pallas import tpu as pltpu
from jax.sharding import PartitionSpec as P

CAP = 2
CHUNKS = 4
LOG2E = 1.4426950408889634
MESH = pl.DeviceIdType.MESH


def shift_order(ny, nz, nc):
    near = [(0, 1), (0, 3), (1, 0), (3, 0)]
    diagonal = [(1, 1), (3, 3), (1, 3), (3, 1)]
    far = [(2, 1), (2, 3), (1, 2), (3, 2)]
    straight = [(2, 0), (0, 2), (2, 2)]
    shifts = [(a, b, c) for c in range(nc) for a, b in straight + far + diagonal + near]
    return shifts + [(0, 0, c) for c in range(1, nc)]


def index_tables(count, source, place_of, partner, ranks, table, req):
    n = source.shape[1]
    down = lax.broadcasted_iota(jnp.int32, (n, n), 0)
    along = lax.broadcasted_iota(jnp.int32, (n, n), 1)

    def upright(row):
        return jnp.sum(jnp.where(down == along, row, 0), axis=1, keepdims=True)

    row = source[...]
    column = upright(row)
    same = column == row
    target = row * CAP + jnp.sum(jnp.where(same & (down < along), 1, 0), axis=0, keepdims=True)
    upright_target = column * CAP + jnp.sum(
        jnp.where(same & (along < down), 1, 0), axis=1, keepdims=True
    )
    hits = upright_target == lax.broadcasted_iota(jnp.int32, (n, 128), 1)
    pair = lax.broadcasted_iota(jnp.int32, (n, 128), 0)
    position = lax.broadcasted_iota(jnp.int32, (1, n), 1)
    table[...] = jnp.zeros_like(table)
    table[0, :, 0:n] = target
    table[1, :, 0:n] = place_of[...]
    table[2, :, 0:n] = jnp.where(position < count[0], ranks[...], 0)
    table[3] = jnp.sum(jnp.where(hits, pair - n, 0), axis=0, keepdims=True) + n
    req[...] = jnp.sum(jnp.where(hits, upright(partner[...]), 0), axis=0, keepdims=True)


def kernel(
    dims,
    count,
    source_in,
    place_in,
    partner_in,
    ranks_in,
    points,
    row_sketch,
    col_sketch,
    row_out,
    col_out,
    pts,
    rsk,
    csk,
    source,
    place_of,
    partner,
    ranks,
    table,
    idx,
    req,
    asked_v,
    asked_s,
    osend,
    left,
    lnorm,
    acc,
    rowv,
    *rest,
):
    groups, subs, own, strip, rank, chunks = dims
    rows = strip // chunks
    pairs = own * subs
    slots = groups * CAP
    send1, recv1, send2, right, col3, rcol, send4 = (
        rest[k * chunks : (k + 1) * chunks] for k in range(7)
    )
    (
        in_sem,
        out_sem,
        local_sem,
        idx_ssem,
        idx_rsem,
        own_ssem,
        own_rsem,
        far1_ssem,
        far1_rsem,
        x2_ssem,
        x2_rsem,
        x3_ssem,
        x3_rsem,
        far4_ssem,
        far4_rsem,
    ) = rest[7 * chunks :]
    me = lax.axis_index("clu")
    sub = lax.axis_index("sub")
    y, z, core = me // 8, lax.rem(me // 2, 4), lax.rem(me, 2)
    shifts = shift_order(4, 4, 2)
    peers = [
        (lax.rem(y + a, 4) * 4 + lax.rem(z + b, 4)) * 2 + lax.rem(core + c, 2) for a, b, c in shifts
    ]
    turns = [2, 1, 3]
    mates = [lax.rem(sub + k, subs) for k in turns]

    loads = [
        pltpu.make_async_copy(points, pts, in_sem.at[0]),
        pltpu.make_async_copy(row_sketch, rsk, in_sem.at[1]),
        pltpu.make_async_copy(col_sketch, csk, in_sem.at[2]),
    ]
    lists = [
        pltpu.make_async_copy(given, held, in_sem.at[5 + k])
        for k, (given, held) in enumerate(
            [(source_in, source), (place_in, place_of), (partner_in, partner), (ranks_in, ranks)]
        )
    ]
    for copy in lists + loads:
        copy.start()
    barrier = pltpu.get_barrier_semaphore()
    for peer in peers:
        pl.semaphore_signal(barrier, inc=1, device_id={"clu": peer}, device_id_type=MESH)
    for mate in mates:
        pl.semaphore_signal(barrier, inc=1, device_id={"sub": mate}, device_id_type=MESH)
    for copy in lists:
        copy.wait()
    index_tables(count, source, place_of, partner, ranks, table, req)
    to_scalar = pltpu.make_async_copy(table, idx, in_sem.at[3])
    to_scalar.start()
    to_scalar.wait()
    loads[0].wait()

    def pick_owner(p, carry):
        osend[p // own, lax.rem(p, own)] = pts[idx[1, 0, p]]
        return carry

    lax.fori_loop(0, pairs, pick_owner, 0)
    pl.semaphore_wait(barrier, len(peers) + len(mates))

    def send(src, dst, ssem, rsem, axis, to):
        pltpu.make_async_remote_copy(
            src_ref=src,
            dst_ref=dst,
            send_sem=ssem,
            recv_sem=rsem,
            device_id={axis: to},
            device_id_type=MESH,
        ).start()

    def await_all(ref, count, sem):
        blocks = ref.at[pl.ds(0, count)]
        pltpu.make_async_copy(blocks, blocks, sem).wait()

    for peer in peers:
        send(req, asked_v.at[me], idx_ssem, idx_rsem, "clu", peer)
    asked_v[me] = req[...]

    for mate in mates:
        send(osend.at[mate], left.at[sub], own_ssem, own_rsem, "sub", mate)
    left[sub] = osend[sub]

    await_all(asked_v, groups - 1, idx_rsem)
    to_scalar = pltpu.make_async_copy(asked_v, asked_s, in_sem.at[4])
    to_scalar.start()
    to_scalar.wait()

    local = []

    def launch(j):
        def wanted(group, c):
            return pts[asked_s[group, 0, me * CAP + c], pl.ds(j * rows, rows)]

        for peer in peers:
            for c in range(CAP):
                send1[j][peer * CAP + c] = wanted(peer, c)
            send(
                send1[j].at[pl.ds(peer * CAP, CAP)],
                recv1[j].at[pl.ds(me * CAP, CAP)],
                far1_ssem.at[j],
                far1_rsem.at[j],
                "clu",
                peer,
            )
        for c in range(CAP):
            recv1[j][me * CAP + c] = wanted(me, c)
        rcol[j][pairs] = jnp.zeros((rows, rank), jnp.bfloat16)

    def norms():
        await_all(left, subs - 1, own_rsem)
        for copy in loads[1:]:
            copy.wait()

        def norms_of(i, carry):
            u = left[:, i].reshape(subs * strip, -1).astype(jnp.float32)
            lnorm[i] = lax.dot_general(
                jnp.ones((8, u.shape[1]), jnp.float32),
                u * u * (LOG2E / u.shape[1]),
                (((1,), (1,)), ((), ())),
                precision=lax.Precision.HIGHEST,
                preferred_element_type=jnp.float32,
            )
            return carry

        lax.fori_loop(0, own, norms_of, 0)

    def forward(j):
        await_all(recv1[j], slots - CAP, far1_rsem.at[j])

        def pick(p, carry):
            send2[j][p // own, lax.rem(p, own)] = recv1[j][idx[0, 0, p]]
            return carry

        lax.fori_loop(0, pairs, pick, 0)
        for mate in mates:
            send(send2[j].at[mate], right[j].at[sub], x2_ssem.at[j], x2_rsem.at[j], "sub", mate)
        right[j][sub] = send2[j][sub]

    def compute(j):
        await_all(right[j], subs - 1, x2_rsem.at[j])

        def one(i, carry):
            u = left[:, i].reshape(subs * strip, -1)
            v = right[j][:, i].reshape(subs * rows, -1)
            width = u.shape[1]
            inner = lax.dot_general(
                v, u, (((1,), (1,)), ((), ())), preferred_element_type=jnp.float32
            )
            wide = v.astype(jnp.float32)
            vnorm = jnp.sum(wide * wide, axis=1, keepdims=True) * (LOG2E / width)
            tile = jnp.exp2(inner * (2.0 * LOG2E / width) - lnorm[i][0:1] - vnorm)
            tile = tile.astype(jnp.bfloat16)
            live = idx[2, 0, sub * own + i]
            keep = (lax.broadcasted_iota(jnp.int32, (1, rank), 1) < live).astype(jnp.float32)
            col = jnp.dot(tile, csk[i], preferred_element_type=jnp.float32) * keep
            col3[j][:, i] = col.astype(jnp.bfloat16).reshape(subs, rows, rank)
            side = rsk[i].reshape(subs, strip, rank)[:, j * rows : (j + 1) * rows]
            part = lax.dot_general(
                tile,
                side.reshape(subs * rows, rank),
                (((0,), (0,)), ((), ())),
                preferred_element_type=jnp.float32,
            )
            if j == 0:
                acc[i] = part
            elif j < chunks - 1:
                acc[i] += part
            else:
                rowv[i] = ((acc[i] + part) * keep).astype(jnp.bfloat16)
            return carry

        lax.fori_loop(0, own, one, 0)
        for mate in mates:
            send(
                col3[j].at[mate],
                rcol[j].at[pl.ds(sub * own, own)],
                x3_ssem.at[j],
                x3_rsem.at[j],
                "sub",
                mate,
            )
        rcol[j][pl.ds(sub * own, own)] = col3[j][sub]

    def give_back(j):
        await_all(rcol[j], pairs - own, x3_rsem.at[j])

        place = pl.ds(j * rows, rows)
        for peer in peers:
            for c in range(CAP):
                send4[j][peer, c] = rcol[j][idx[3, 0, peer * CAP + c]]
            send(
                send4[j].at[peer],
                col_out.at[me, :, place],
                far4_ssem.at[j],
                far4_rsem,
                "clu",
                peer,
            )
        for c in range(CAP):
            send4[j][me, c] = rcol[j][idx[3, 0, me * CAP + c]]
        mine = pltpu.make_async_copy(send4[j].at[me], col_out.at[me, :, place], local_sem.at[j])
        mine.start()
        local.append(mine)

    for j in range(chunks):
        launch(j)
    norms()
    forward(0)
    for j in range(chunks):
        if j + 1 < chunks:
            forward(j + 1)
        compute(j)
        if j > 0:
            give_back(j - 1)
    store = pltpu.make_async_copy(rowv, row_out, out_sem)
    store.start()
    give_back(chunks - 1)

    await_all(asked_v, groups - 1, idx_ssem)
    await_all(left, subs - 1, own_ssem)
    for j in range(chunks):
        await_all(send1[j], slots - CAP, far1_ssem.at[j])
        await_all(send2[j], subs - 1, x2_ssem.at[j])
        await_all(col3[j], subs - 1, x3_ssem.at[j])
        await_all(send4[j], groups - 1, far4_ssem.at[j])
    await_all(col_out, groups - 1, far4_rsem)
    for copy in local:
        copy.wait()
    store.wait()


def shards(
    points, row_sketch, col_sketch, pair_count, pair_local, pair_src, pair_partner, pair_rank
):
    groups = lax.axis_size("clu")
    subs = lax.axis_size("sub")
    clusters, strip, width = points.shape
    pairs = pair_src.shape[1]
    own = pairs // subs
    rank = row_sketch.shape[3]
    chunks = CHUNKS
    rows = strip // chunks
    slots = groups * CAP

    per_chunk = [
        ((slots, rows, width), jnp.bfloat16),
        ((slots, rows, width), jnp.bfloat16),
        ((subs, own, rows, width), jnp.bfloat16),
        ((subs, own, rows, width), jnp.bfloat16),
        ((subs, own, rows, rank), jnp.bfloat16),
        ((pairs + 1, rows, rank), jnp.bfloat16),
        ((groups, CAP, rows, rank), jnp.bfloat16),
    ]
    scratch = [
        pltpu.VMEM((clusters, strip, width), jnp.bfloat16),
        pltpu.VMEM((own, subs * strip, rank), jnp.bfloat16),
        pltpu.VMEM((own, subs * strip, rank), jnp.bfloat16),
        pltpu.VMEM((1, pairs), jnp.int32),
        pltpu.VMEM((1, pairs), jnp.int32),
        pltpu.VMEM((1, pairs), jnp.int32),
        pltpu.VMEM((1, pairs), jnp.int32),
        pltpu.VMEM((4, 1, 128), jnp.int32),
        pltpu.SMEM((4, 1, 128), jnp.int32),
        pltpu.VMEM((1, 128), jnp.int32),
        pltpu.VMEM((groups, 1, 128), jnp.int32),
        pltpu.SMEM((groups, 1, 128), jnp.int32),
        pltpu.VMEM((subs, own, strip, width), jnp.bfloat16),
        pltpu.VMEM((subs, own, strip, width), jnp.bfloat16),
        pltpu.VMEM((own, 8, subs * strip), jnp.float32),
        pltpu.VMEM((own, subs * strip, rank), jnp.float32),
        pltpu.VMEM((own, subs * strip, rank), jnp.bfloat16),
    ]
    for shape, dtype in per_chunk:
        scratch += [pltpu.VMEM(shape, dtype) for _ in range(chunks)]
    dma = pltpu.SemaphoreType.DMA
    scratch += [
        dma((9,)),
        dma,
        dma((chunks,)),
        dma,
        dma,
        dma,
        dma,
        dma((chunks,)),
        dma((chunks,)),
        dma((chunks,)),
        dma((chunks,)),
        dma((chunks,)),
        dma((chunks,)),
        dma((chunks,)),
        dma,
    ]
    anywhere = pl.BlockSpec(memory_space=pl.ANY)
    row, col = pl.pallas_call(
        functools.partial(kernel, (groups, subs, own, strip, rank, chunks)),
        out_shape=(
            jax.ShapeDtypeStruct((own, subs * strip, rank), jnp.bfloat16),
            jax.ShapeDtypeStruct((groups, CAP, strip, rank), jnp.bfloat16),
        ),
        in_specs=[
            pl.BlockSpec(memory_space=pltpu.SMEM),
            anywhere,
            anywhere,
            anywhere,
            anywhere,
            anywhere,
            anywhere,
            anywhere,
        ],
        out_specs=(anywhere, anywhere),
        scratch_shapes=scratch,
        compiler_params=pltpu.CompilerParams(
            collective_id=0, has_side_effects=True, vmem_limit_bytes=56 << 20
        ),
        name="pair_sketches",
    )(
        pair_count,
        pair_src,
        pair_local,
        pair_partner,
        pair_rank,
        points,
        row_sketch[0],
        col_sketch[0],
    )
    return row[None], col[None]


def solution(mesh):
    placed = (
        P("clu", "sub", None),
        P("clu", "sub", None, None),
        P("clu", "sub", None, None),
        P("clu"),
        P("clu", None),
        P("clu", None),
        P("clu", None),
        P("clu", None),
    )
    return jax.shard_map(
        shards,
        mesh=mesh,
        in_specs=placed,
        out_specs=(P("clu", "sub", None, None), P("clu", None, None, "sub", None)),
        check_vma=False,
    )
```

```python
import functools

import jax
import jax.numpy as jnp
from jax import lax
from jax.experimental import pallas as pl
from jax.experimental.pallas import tpu as pltpu
from jax.sharding import PartitionSpec as P

CAP = 2
CHUNKS = 8
LOG2E = 1.4426950408889634
MESH = pl.DeviceIdType.MESH


def shift_order(ny, nz, nc):
    near = [(0, 1), (0, 3), (1, 0), (3, 0)]
    diagonal = [(1, 1), (3, 3), (1, 3), (3, 1)]
    far = [(2, 1), (2, 3), (1, 2), (3, 2)]
    straight = [(2, 0), (0, 2), (2, 2)]
    shifts = [(a, b, c) for c in range(nc) for a, b in straight + far + diagonal + near]
    return shifts + [(0, 0, c) for c in range(1, nc)]


def index_tables(count, source, place_of, partner, ranks, table, req):
    n = source.shape[1]
    down = lax.broadcasted_iota(jnp.int32, (n, n), 0)
    along = lax.broadcasted_iota(jnp.int32, (n, n), 1)

    def upright(row):
        return jnp.sum(jnp.where(down == along, row, 0), axis=1, keepdims=True)

    row = source[...]
    column = upright(row)
    same = column == row
    target = row * CAP + jnp.sum(jnp.where(same & (down < along), 1, 0), axis=0, keepdims=True)
    upright_target = column * CAP + jnp.sum(
        jnp.where(same & (along < down), 1, 0), axis=1, keepdims=True
    )
    hits = upright_target == lax.broadcasted_iota(jnp.int32, (n, 128), 1)
    pair = lax.broadcasted_iota(jnp.int32, (n, 128), 0)
    position = lax.broadcasted_iota(jnp.int32, (1, n), 1)
    table[...] = jnp.zeros_like(table)
    table[0, :, 0:n] = target
    table[1, :, 0:n] = place_of[...]
    table[2, :, 0:n] = jnp.where(position < count[0], ranks[...], 0)
    table[3] = jnp.sum(jnp.where(hits, pair - n, 0), axis=0, keepdims=True) + n
    req[...] = jnp.sum(jnp.where(hits, upright(partner[...]), 0), axis=0, keepdims=True)


def kernel(
    dims,
    count,
    source_in,
    place_in,
    partner_in,
    ranks_in,
    points,
    row_sketch,
    col_sketch,
    row_out,
    col_out,
    pts,
    rsk,
    csk,
    source,
    place_of,
    partner,
    ranks,
    table,
    idx,
    req,
    asked_v,
    asked_s,
    osend,
    left,
    lnorm,
    acc,
    rowv,
    *rest,
):
    groups, subs, own, strip, rank, chunks = dims
    rows = strip // chunks
    pairs = own * subs
    slots = groups * CAP
    send1, recv1, send2, right, col3, rcol, send4 = (
        rest[k * chunks : (k + 1) * chunks] for k in range(7)
    )
    (
        in_sem,
        out_sem,
        local_sem,
        idx_ssem,
        idx_rsem,
        own_ssem,
        own_rsem,
        far1_ssem,
        far1_rsem,
        x2_ssem,
        x2_rsem,
        x3_ssem,
        x3_rsem,
        far4_ssem,
        far4_rsem,
    ) = rest[7 * chunks :]
    me = lax.axis_index("clu")
    sub = lax.axis_index("sub")
    y, z, core = me // 8, lax.rem(me // 2, 4), lax.rem(me, 2)
    shifts = shift_order(4, 4, 2)
    peers = [
        (lax.rem(y + a, 4) * 4 + lax.rem(z + b, 4)) * 2 + lax.rem(core + c, 2) for a, b, c in shifts
    ]
    turns = [2, 1, 3]
    mates = [lax.rem(sub + k, subs) for k in turns]

    loads = [
        pltpu.make_async_copy(points, pts, in_sem.at[0]),
        pltpu.make_async_copy(row_sketch, rsk, in_sem.at[1]),
        pltpu.make_async_copy(col_sketch, csk, in_sem.at[2]),
    ]
    lists = [
        pltpu.make_async_copy(given, held, in_sem.at[5 + k])
        for k, (given, held) in enumerate(
            [(source_in, source), (place_in, place_of), (partner_in, partner), (ranks_in, ranks)]
        )
    ]
    for copy in lists + loads:
        copy.start()
    barrier = pltpu.get_barrier_semaphore()
    for peer in peers:
        pl.semaphore_signal(barrier, inc=1, device_id={"clu": peer}, device_id_type=MESH)
    for mate in mates:
        pl.semaphore_signal(barrier, inc=1, device_id={"sub": mate}, device_id_type=MESH)
    for copy in lists:
        copy.wait()
    index_tables(count, source, place_of, partner, ranks, table, req)
    to_scalar = pltpu.make_async_copy(table, idx, in_sem.at[3])
    to_scalar.start()
    to_scalar.wait()
    loads[0].wait()

    def pick_owner(p, carry):
        osend[p // own, lax.rem(p, own)] = pts[idx[1, 0, p]]
        return carry

    lax.fori_loop(0, pairs, pick_owner, 0)
    pl.semaphore_wait(barrier, len(peers) + len(mates))

    def send(src, dst, ssem, rsem, axis, to):
        pltpu.make_async_remote_copy(
            src_ref=src,
            dst_ref=dst,
            send_sem=ssem,
            recv_sem=rsem,
            device_id={axis: to},
            device_id_type=MESH,
        ).start()

    def await_all(ref, count, sem):
        blocks = ref.at[pl.ds(0, count)]
        pltpu.make_async_copy(blocks, blocks, sem).wait()

    for peer in peers:
        send(req, asked_v.at[me], idx_ssem, idx_rsem, "clu", peer)
    asked_v[me] = req[...]

    for mate in mates:
        send(osend.at[mate], left.at[sub], own_ssem, own_rsem, "sub", mate)
    left[sub] = osend[sub]

    await_all(asked_v, groups - 1, idx_rsem)
    to_scalar = pltpu.make_async_copy(asked_v, asked_s, in_sem.at[4])
    to_scalar.start()
    to_scalar.wait()

    local = []

    def launch(j):
        def wanted(group, c):
            return pts[asked_s[group, 0, me * CAP + c], pl.ds(j * rows, rows)]

        for peer in peers:
            for c in range(CAP):
                send1[j][peer * CAP + c] = wanted(peer, c)
            send(
                send1[j].at[pl.ds(peer * CAP, CAP)],
                recv1[j].at[pl.ds(me * CAP, CAP)],
                far1_ssem.at[j],
                far1_rsem.at[j],
                "clu",
                peer,
            )
        for c in range(CAP):
            recv1[j][me * CAP + c] = wanted(me, c)
        rcol[j][pairs] = jnp.zeros((rows, rank), jnp.bfloat16)

    def norms():
        await_all(left, subs - 1, own_rsem)
        for copy in loads[1:]:
            copy.wait()

        def norms_of(i, carry):
            u = left[:, i].reshape(subs * strip, -1).astype(jnp.float32)
            lnorm[i] = lax.dot_general(
                jnp.ones((8, u.shape[1]), jnp.float32),
                u * u * (LOG2E / u.shape[1]),
                (((1,), (1,)), ((), ())),
                precision=lax.Precision.HIGHEST,
                preferred_element_type=jnp.float32,
            )
            return carry

        lax.fori_loop(0, own, norms_of, 0)

    def forward(j):
        await_all(recv1[j], slots - CAP, far1_rsem.at[j])

        def pick(p, carry):
            send2[j][p // own, lax.rem(p, own)] = recv1[j][idx[0, 0, p]]
            return carry

        lax.fori_loop(0, pairs, pick, 0)
        for mate in mates:
            send(send2[j].at[mate], right[j].at[sub], x2_ssem.at[j], x2_rsem.at[j], "sub", mate)
        right[j][sub] = send2[j][sub]

    def compute(j):
        await_all(right[j], subs - 1, x2_rsem.at[j])

        def one(i, carry):
            u = left[:, i].reshape(subs * strip, -1)
            v = right[j][:, i].reshape(subs * rows, -1)
            width = u.shape[1]
            inner = lax.dot_general(
                v, u, (((1,), (1,)), ((), ())), preferred_element_type=jnp.float32
            )
            wide = v.astype(jnp.float32)
            vnorm = jnp.sum(wide * wide, axis=1, keepdims=True) * (LOG2E / width)
            tile = jnp.exp2(inner * (2.0 * LOG2E / width) - lnorm[i][0:1] - vnorm)
            tile = tile.astype(jnp.bfloat16)
            live = idx[2, 0, sub * own + i]
            keep = (lax.broadcasted_iota(jnp.int32, (1, rank), 1) < live).astype(jnp.float32)
            col = jnp.dot(tile, csk[i], preferred_element_type=jnp.float32) * keep
            col3[j][:, i] = col.astype(jnp.bfloat16).reshape(subs, rows, rank)
            side = rsk[i].reshape(subs, strip, rank)[:, j * rows : (j + 1) * rows]
            part = lax.dot_general(
                tile,
                side.reshape(subs * rows, rank),
                (((0,), (0,)), ((), ())),
                preferred_element_type=jnp.float32,
            )
            if j == 0:
                acc[i] = part
            elif j < chunks - 1:
                acc[i] += part
            else:
                rowv[i] = ((acc[i] + part) * keep).astype(jnp.bfloat16)
            return carry

        lax.fori_loop(0, own, one, 0)
        for mate in mates:
            send(
                col3[j].at[mate],
                rcol[j].at[pl.ds(sub * own, own)],
                x3_ssem.at[j],
                x3_rsem.at[j],
                "sub",
                mate,
            )
        rcol[j][pl.ds(sub * own, own)] = col3[j][sub]

    def give_back(j):
        await_all(rcol[j], pairs - own, x3_rsem.at[j])

        place = pl.ds(j * rows, rows)
        for peer in peers:
            for c in range(CAP):
                send4[j][peer, c] = rcol[j][idx[3, 0, peer * CAP + c]]
            send(
                send4[j].at[peer],
                col_out.at[me, :, place],
                far4_ssem.at[j],
                far4_rsem,
                "clu",
                peer,
            )
        for c in range(CAP):
            send4[j][me, c] = rcol[j][idx[3, 0, me * CAP + c]]
        mine = pltpu.make_async_copy(send4[j].at[me], col_out.at[me, :, place], local_sem.at[j])
        mine.start()
        local.append(mine)

    for j in range(chunks):
        launch(j)
    norms()
    forward(0)
    forward(1)
    for j in range(chunks):
        if j + 2 < chunks:
            forward(j + 2)
        compute(j)
        if j > 0:
            give_back(j - 1)
    store = pltpu.make_async_copy(rowv, row_out, out_sem)
    store.start()
    give_back(chunks - 1)

    await_all(asked_v, groups - 1, idx_ssem)
    await_all(left, subs - 1, own_ssem)
    for j in range(chunks):
        await_all(send1[j], slots - CAP, far1_ssem.at[j])
        await_all(send2[j], subs - 1, x2_ssem.at[j])
        await_all(col3[j], subs - 1, x3_ssem.at[j])
        await_all(send4[j], groups - 1, far4_ssem.at[j])
    await_all(col_out, groups - 1, far4_rsem)
    for copy in local:
        copy.wait()
    store.wait()


def shards(
    points, row_sketch, col_sketch, pair_count, pair_local, pair_src, pair_partner, pair_rank
):
    groups = lax.axis_size("clu")
    subs = lax.axis_size("sub")
    clusters, strip, width = points.shape
    pairs = pair_src.shape[1]
    own = pairs // subs
    rank = row_sketch.shape[3]
    chunks = CHUNKS
    rows = strip // chunks
    slots = groups * CAP

    per_chunk = [
        ((slots, rows, width), jnp.bfloat16),
        ((slots, rows, width), jnp.bfloat16),
        ((subs, own, rows, width), jnp.bfloat16),
        ((subs, own, rows, width), jnp.bfloat16),
        ((subs, own, rows, rank), jnp.bfloat16),
        ((pairs + 1, rows, rank), jnp.bfloat16),
        ((groups, CAP, rows, rank), jnp.bfloat16),
    ]
    scratch = [
        pltpu.VMEM((clusters, strip, width), jnp.bfloat16),
        pltpu.VMEM((own, subs * strip, rank), jnp.bfloat16),
        pltpu.VMEM((own, subs * strip, rank), jnp.bfloat16),
        pltpu.VMEM((1, pairs), jnp.int32),
        pltpu.VMEM((1, pairs), jnp.int32),
        pltpu.VMEM((1, pairs), jnp.int32),
        pltpu.VMEM((1, pairs), jnp.int32),
        pltpu.VMEM((4, 1, 128), jnp.int32),
        pltpu.SMEM((4, 1, 128), jnp.int32),
        pltpu.VMEM((1, 128), jnp.int32),
        pltpu.VMEM((groups, 1, 128), jnp.int32),
        pltpu.SMEM((groups, 1, 128), jnp.int32),
        pltpu.VMEM((subs, own, strip, width), jnp.bfloat16),
        pltpu.VMEM((subs, own, strip, width), jnp.bfloat16),
        pltpu.VMEM((own, 8, subs * strip), jnp.float32),
        pltpu.VMEM((own, subs * strip, rank), jnp.float32),
        pltpu.VMEM((own, subs * strip, rank), jnp.bfloat16),
    ]
    for shape, dtype in per_chunk:
        scratch += [pltpu.VMEM(shape, dtype) for _ in range(chunks)]
    dma = pltpu.SemaphoreType.DMA
    scratch += [
        dma((9,)),
        dma,
        dma((chunks,)),
        dma,
        dma,
        dma,
        dma,
        dma((chunks,)),
        dma((chunks,)),
        dma((chunks,)),
        dma((chunks,)),
        dma((chunks,)),
        dma((chunks,)),
        dma((chunks,)),
        dma,
    ]
    anywhere = pl.BlockSpec(memory_space=pl.ANY)
    row, col = pl.pallas_call(
        functools.partial(kernel, (groups, subs, own, strip, rank, chunks)),
        out_shape=(
            jax.ShapeDtypeStruct((own, subs * strip, rank), jnp.bfloat16),
            jax.ShapeDtypeStruct((groups, CAP, strip, rank), jnp.bfloat16),
        ),
        in_specs=[
            pl.BlockSpec(memory_space=pltpu.SMEM),
            anywhere,
            anywhere,
            anywhere,
            anywhere,
            anywhere,
            anywhere,
            anywhere,
        ],
        out_specs=(anywhere, anywhere),
        scratch_shapes=scratch,
        compiler_params=pltpu.CompilerParams(
            collective_id=0, has_side_effects=True, vmem_limit_bytes=56 << 20
        ),
        name="pair_sketches",
    )(
        pair_count,
        pair_src,
        pair_local,
        pair_partner,
        pair_rank,
        points,
        row_sketch[0],
        col_sketch[0],
    )
    return row[None], col[None]


def solution(mesh):
    placed = (
        P("clu", "sub", None),
        P("clu", "sub", None, None),
        P("clu", "sub", None, None),
        P("clu"),
        P("clu", None),
        P("clu", None),
        P("clu", None),
        P("clu", None),
    )
    return jax.shard_map(
        shards,
        mesh=mesh,
        in_specs=placed,
        out_specs=(P("clu", "sub", None, None), P("clu", None, None, "sub", None)),
        check_vma=False,
    )
```
